32 devices in a mesh: song: 2 (over x), tm: 8 (over z, y), freq: 2 (over core).
Axes of the slice: x: 2, y: 2, z: 4, core: 2. Of those that a mesh axis runs over, the one named last changes fastest.
Arguments:
- latent: bfloat16 [256, 128, 1024], P(None, 'freq', ('song', 'tm')), parts along dimension 2, as said below
- mel_noisy: float32 [128, 1024], P('freq', ('song', 'tm')), parts along dimension 1, may hold values from -6 to 6
- time_shift: float32 [512], P('song'), parts along dimension 0, may hold values from -3 to 3
- first_gain: float32 [256], replicated, may hold values from 0.5 to 1.5
- first_shift: float32 [256], replicated, may hold values from -3 to 3
- conv_first: bfloat16 [3, 3, 256, 256], replicated, may hold values from -0.125 to 0.125
- second_gain: float32 [256], replicated, may hold values from 0.5 to 1.5
- second_shift: float32 [256], replicated, may hold values from -3 to 3
- conv_second: bfloat16 [3, 3, 256, 256], replicated, may hold values from -0.125 to 0.125
- second_bias: float32 [256], replicated, may hold values from -3 to 3
- out_proj: float32 [256], replicated, may hold values from -0.375 to 0.375
- pre_weight: bfloat16 [1536, 7, 128], P('tm'), may hold values from -0.1875 to 0.1875
- pre_bias: float32 [1536], replicated, may hold values from -3 to 3
- up_weight: bfloat16 [1536, 8, 768], P(None, None, 'freq'), may hold values from -0.109375 to 0.109375
- up_bias: float32 [768], P('freq'), may hold values from -3 to 3
Outputs:
- mel_next: float32 [128, 1024], P('freq', ('song', 'tm')), parts along dimension 1
- vocal: bfloat16 [768, 4096], P('freq', ('song', 'tm')), parts along dimension 1
The draws below stay inside these ranges and needn't reach their ends.
There are 2 independent parts, one for each index of `song`. The reference program is written for one: setup_inputs(seed, part) draws one part's arguments, and reference() takes and returns one part's arrays. A program takes and returns all parts, laid end to end along the dimension named above; an argument that names none is the same for every part. Nothing has to cross between parts.
Inputs may be any that keep to these rules, and one draw needn't show every extreme that they name: `latent`: activations of the block's input, of order one to some tens.
All inputs are finite; a program needn't handle non-finite values.
Results may differ from the reference program's by a relative error of at most 0.0055.
Values may be sent and summed in bfloat16 or wider, within the bound.
No kernel may reach another device: no remote copies, remote signals or barrier semaphores. Data moves between devices by JAX's collectives and lax.ppermute only.
A program may use at most 192 MiB of HBM per device.

```python
import jax
import jax.numpy as jnp
from jax import lax

CHANNELS = 256
MELS = 128
GROUPS = 32
PRE_WIDTH = 1536
UP_WIDTH = 768
FRAMES = 512


def draw_latent(key, part):
    key_base, key_chan, key_frame = jax.random.split(key, 3)
    base = jnp.clip(jax.random.normal(key_base, (CHANNELS, MELS, FRAMES), jnp.float32), -5.0, 5.0)
    ramp = 3.0 ** (jnp.arange(FRAMES, dtype=jnp.float32) / FRAMES - 0.5)
    chan_scale = 10.0 ** (jax.random.uniform(key_chan, (CHANNELS,), jnp.float32) - 0.5)
    rough = jax.random.uniform(key_frame, (FRAMES,), jnp.float32, 0.5, 2.0)
    values = base * chan_scale[:, None, None] * (rough * ramp)[None, None, :]
    return values.astype(jnp.bfloat16)


def steps_of(key, dims, pieces, least, top_value):
    level, own = 1.0, jax.random.fold_in(key, 6)
    for position, shards_of in pieces:
        heights = jnp.exp(jax.random.uniform(jax.random.fold_in(own, position), (shards_of,), jnp.float32, least / len(pieces), top_value / len(pieces)))
        level = level * jnp.repeat(heights, dims[position] // shards_of).reshape([-1 if axis == position else 1 for axis in range(len(dims))])
    return level


def normal_values(rng, shape, spread, reach, pieces=(), kind=jnp.bfloat16):
    array = jax.random.normal(rng, shape, jnp.float32) * spread
    if len(pieces) > 0:
        array = steps_of(rng, shape, pieces, -0.22, 0.18) * array
    return jnp.clip(array, min=-reach, max=reach).astype(kind)


def setup_inputs(seed: int = 0, part: int = 0) -> dict:
    key_of = jax.random.split(jax.random.key(seed), 16)
    part_splits = jax.random.split(jax.random.fold_in(key_of[15], part), 16)
    return {
        "latent": draw_latent(jax.random.fold_in(jax.random.fold_in(key_of[15], part), 71), part),
        "mel_noisy": normal_values(part_splits[1], (MELS, FRAMES), 1.0, 6.0, ((0, 2), (1, 8)), jnp.float32),
        "time_shift": normal_values(part_splits[2], (CHANNELS,), 0.5, 3.0, (), jnp.float32),
        "first_gain": jnp.clip(jax.random.uniform(key_of[3], (CHANNELS,), jnp.float32, 0.5, 1.5), 0.5, 1.5),
        "first_shift": normal_values(key_of[4], (CHANNELS,), 0.5, 3.0, (), jnp.float32),
        "conv_first": normal_values(key_of[5], (3, 3, CHANNELS, CHANNELS), (9 * CHANNELS) ** -0.5, 0.125),
        "second_gain": jnp.clip(jax.random.uniform(key_of[6], (CHANNELS,), jnp.float32, 0.5, 1.5), 0.5, 1.5),
        "second_shift": normal_values(key_of[7], (CHANNELS,), 0.5, 3.0, (), jnp.float32),
        "conv_second": normal_values(key_of[8], (3, 3, CHANNELS, CHANNELS), (9 * CHANNELS) ** -0.5, 0.125),
        "second_bias": normal_values(key_of[9], (CHANNELS,), 0.5, 3.0, (), jnp.float32),
        "out_proj": normal_values(key_of[10], (CHANNELS,), CHANNELS ** -0.5, 0.375, (), jnp.float32),
        "pre_weight": normal_values(key_of[11], (PRE_WIDTH, 7, MELS), (7 * MELS) ** -0.5, 0.1875, ((0, 8),)),
        "pre_bias": normal_values(key_of[12], (PRE_WIDTH,), 0.5, 3.0, (), jnp.float32),
        "up_weight": normal_values(key_of[13], (PRE_WIDTH, 8, UP_WIDTH), (2 * PRE_WIDTH) ** -0.5, 0.109375, ((2, 2),)),
        "up_bias": normal_values(key_of[14], (UP_WIDTH,), 0.5, 3.0, ((0, 2),), jnp.float32),
    }


EPSILON = 1e-05
STEP_SIZE = 0.25

def norm_silu(values_in, gain, shift):
    chans, bins, frames = values_in.shape
    values = values_in.astype(jnp.float32).reshape(GROUPS, chans // GROUPS, bins, frames)
    count = float(chans // GROUPS * bins * frames)
    mean = lax.optimization_barrier(jnp.sum(values, axis=(1, 2, 3))) / count
    var = lax.optimization_barrier(jnp.sum(values * values, axis=(1, 2, 3))) / count - mean * mean
    scaled = (values - mean[:, None, None, None]) * lax.rsqrt(var + EPSILON)[:, None, None, None]
    scaled = scaled.reshape(chans, bins, frames) * gain[:, None, None] + shift[:, None, None]
    return jax.nn.silu(scaled).astype(jnp.bfloat16)

def conv_three(active, weight):
    bins, frames = (active.shape[1], active.shape[2])
    padded = jnp.pad(active.astype(jnp.float32), ((0, 0), (1, 1), (1, 1)))
    wide = weight.astype(jnp.float32)
    total = jnp.zeros((weight.shape[3], bins, frames), jnp.float32)
    for i in range(3):
        for j in range(3):
            total = total + jnp.einsum('io,ift->oft', wide[i, j], padded[:, i:i + bins, j:j + frames])
    return total

def up_tap(up_weight, k, feats):
    return jnp.dot(up_weight[:, k, :].T, feats, preferred_element_type=jnp.float32)

def reference(latent, mel_noisy, time_shift, first_gain, first_shift, conv_first, second_gain, second_shift, conv_second, second_bias, out_proj, pre_weight, pre_bias, up_weight, up_bias):
    active = norm_silu(latent, first_gain, first_shift)
    first_out = (conv_three(active, conv_first) + time_shift[:, None, None]).astype(jnp.bfloat16)
    second_in = norm_silu(first_out, second_gain, second_shift)
    hidden = latent.astype(jnp.float32) + conv_three(second_in, conv_second) + second_bias[:, None, None]
    velocity = lax.optimization_barrier(jnp.sum(out_proj[:, None, None] * hidden, axis=0))
    mel_next = mel_noisy + STEP_SIZE * velocity
    mel_in = mel_next.astype(jnp.bfloat16)
    frames = mel_in.shape[1]
    padded = jnp.pad(mel_in, ((0, 0), (3, 3)))
    total = jnp.zeros((pre_weight.shape[0], frames), jnp.float32)
    for k in range(7):
        total = total + jnp.dot(pre_weight[:, k, :], padded[:, k:k + frames], preferred_element_type=jnp.float32)
    features = (total + pre_bias[:, None]).astype(jnp.bfloat16)
    framed = jnp.pad(features, ((0, 0), (1, 1)))
    middle = framed[:, 1:frames + 1]
    before = framed[:, 0:frames]
    after = framed[:, 2:frames + 2]
    phases = []
    for p in range(4):
        term = up_tap(up_weight, p + 2, middle)
        if p <= 1:
            term = term + up_tap(up_weight, p + 6, before)
        else:
            term = term + up_tap(up_weight, p - 2, after)
        phases.append(term)
    stacked = jnp.stack(phases, axis=2).reshape(up_weight.shape[2], 4 * frames)
    vocal = (stacked + up_bias[:, None]).astype(jnp.bfloat16)
    return (mel_next, vocal)
```

```python
import functools

import jax
import jax.numpy as jnp
from jax import lax
from jax.experimental import pallas as pl
from jax.experimental.pallas import tpu as pltpu
from jax.sharding import PartitionSpec as P

GROUPS = 32
EPSILON = 1e-05
STEP_SIZE = 0.25
EDGE = 8
F32 = jnp.float32
BF16 = jnp.bfloat16
VMEM = pl.BlockSpec(memory_space=pltpu.VMEM)
SMEM = pl.BlockSpec(memory_space=pltpu.SMEM)


def nt(a, b):
    return lax.dot_general(a, b, (((1,), (1,)), ((), ())), preferred_element_type=F32)


def split3(x):
    hi = x.astype(BF16)
    rest = x - hi.astype(F32)
    mid = rest.astype(BF16)
    low = (rest - mid.astype(F32)).astype(BF16)
    return hi, mid, low


def norm_terms(stats, gain, count):
    chans = stats.shape[1] // 2
    total = jnp.sum(stats, axis=0, keepdims=True)
    size = chans // GROUPS
    rows = lax.broadcasted_iota(jnp.int32, (chans, chans), 0) // size
    cols = lax.broadcasted_iota(jnp.int32, (chans, chans), 1) // size
    same = jnp.where(rows == cols, 1.0, 0.0).astype(F32)
    both = jnp.concatenate([total[:, :chans], total[:, chans:]], axis=0)
    both = jnp.concatenate([both, jnp.zeros((6, chans), F32)], axis=0)
    groups = lax.dot_general(
        both, same, (((1,), (0,)), ((), ())), precision=lax.Precision.HIGHEST, preferred_element_type=F32
    )
    mean = groups[0:1] / count
    var = groups[1:2] / count - mean * mean
    return mean, lax.rsqrt(var + EPSILON) * gain


def half_silu(values, mean, scale, shift):
    half = (values - mean) * (scale * 0.5) + shift * 0.5
    return half + half * jnp.tanh(half)


def conv_kernel(bins, frames, rows, count, info, stats, gain, shift, tshift, own, left, right, top, bottom,
                weight, proj, out, moments, base, act):
    chans = own.shape[-1]
    width = frames + 2 * EDGE
    tm, tms, fq, fqs = info[0], info[1], info[2], info[3]
    mean, scale = norm_terms(stats[...], gain[...], count)
    shift_v = shift[...]
    place = lax.broadcasted_iota(jnp.int32, (width, 1), 0) - EDGE + tm * frames
    inside = jnp.where((place >= 0) & (place < frames * tms), 1.0, 0.0).astype(F32)
    inside = jnp.broadcast_to(inside, (width, chans))

    def put(row, middle, bin_ok):
        l32, m32, r32 = left[row].astype(F32), middle.astype(F32), right[row].astype(F32)
        raw = jnp.concatenate([l32, m32, r32], axis=0)
        val = half_silu(raw, mean, scale, shift_v)
        keep = inside > 0.0 if bin_ok is None else (inside * bin_ok) > 0.0
        val = jnp.where(keep, val, 0.0)
        act[row, :, 0:chans] = pltpu.roll(val, 1, 0).astype(BF16)
        act[row, :, chans : 2 * chans] = val.astype(BF16)
        act[row, :, 2 * chans : 3 * chans] = pltpu.roll(val, width - 1, 0).astype(BF16)
        return raw

    has_top = jnp.where(fq > 0, 1.0, 0.0).astype(F32)
    has_bottom = jnp.where(fq < fqs - 1, 1.0, 0.0).astype(F32)

    def put_own(i):
        raw = put(i + 2, own[i], None)
        parts = nt(proj[...], raw.astype(BF16))
        base[i] = parts[0:8] + parts[8:16] + parts[16:24]

    put(0, top[0], has_top)
    put(1, top[1], has_top)
    for i in range(rows):
        put_own(i)
    put(bins + 2, bottom[0], has_bottom)
    put(bins + 3, bottom[1], has_bottom)

    blocks = (bins + 2) // rows

    def matmul(b, acc_s, acc_q):
        first = b * rows
        lhs = jnp.concatenate([act[pl.ds(first + i, rows)] for i in range(3)], axis=-1)
        lhs = lhs.reshape(rows * width, 9 * chans)
        res = jnp.dot(lhs, weight[...], preferred_element_type=F32) + tshift[...]
        res = res.reshape(rows, width, chans).astype(BF16)
        out[pl.ds(first, rows)] = res
        for r in range(rows):
            line = first + r
            ok = jnp.where((line >= 1) & (line <= bins), 1.0, 0.0).astype(F32)
            vals = res[r].astype(F32)[EDGE : EDGE + frames] * ok
            vals = vals.reshape(frames // 8, 8, chans)
            acc_s = acc_s + jnp.sum(vals, axis=0)
            acc_q = acc_q + jnp.sum(vals * vals, axis=0)
        return acc_s, acc_q

    def step(b, carry):
        for r in range(rows):
            i = b * rows + rows + r

            @pl.when(i < bins)
            def _():
                put_own(i)

        return matmul(b, *carry)

    zero = jnp.zeros((8, chans), F32)
    acc_s, acc_q = lax.fori_loop(0, blocks, step, (zero, zero))
    moments[0:1, 0:chans] = jnp.sum(acc_s, axis=0, keepdims=True)
    moments[0:1, chans : 2 * chans] = jnp.sum(acc_q, axis=0, keepdims=True)


def mel_kernel(bins, frames, count, info, const, stats, gain, shift, first_out, weights, base, noisy, mel, mel_in, sums):
    chans = first_out.shape[-1]
    width = frames + 2 * EDGE
    tm, tms, fq, fqs = info[0], info[1], info[2], info[3]
    mean, scale = norm_terms(stats[...], gain[...], count)
    shift_v = shift[...]
    place = lax.broadcasted_iota(jnp.int32, (width, 1), 0) - EDGE + tm * frames
    inside = jnp.where((place >= 0) & (place < frames * tms), 1.0, 0.0).astype(F32)
    inside = jnp.broadcast_to(inside, (width, chans))
    sums[...] = jnp.zeros_like(sums)

    def row(r, _):
        bin_ok = ((r > 0) | (fq > 0)) & ((r < bins + 1) | (fq < fqs - 1))
        ok = jnp.where(bin_ok, 1.0, 0.0).astype(F32)
        val = half_silu(first_out[r].astype(F32), mean, scale, shift_v)
        val = jnp.where(inside * ok > 0.0, val, 0.0).astype(BF16)
        taps = nt(weights[...], val)
        taps = taps[0:24] + taps[24:48] + taps[48:72]
        w = width
        sums[pl.ds(pl.multiple_of((r + 2) * 8, 8), 8), 0:w] = taps[0:8]
        at = pl.multiple_of((r + 1) * 8, 8)
        sums[pl.ds(at, 8), 0:w] = sums[pl.ds(at, 8), 0:w] + taps[8:16]
        at = pl.multiple_of(r * 8, 8)
        sums[pl.ds(at, 8), 0:w] = sums[pl.ds(at, 8), 0:w] + taps[16:24]
        return 0

    lax.fori_loop(0, bins + 2, row, 0, unroll=6)
    lanes = sums.shape[1]
    t0 = sums[pl.ds(16, bins, stride=8), :]
    t1 = sums[pl.ds(17, bins, stride=8), :]
    t2 = sums[pl.ds(18, bins, stride=8), :]
    b1 = base[pl.ds(1, bins, stride=8), :]
    vel = pltpu.roll(t0, 1, 1) + t1 + pltpu.roll(t2, lanes - 1, 1)
    vel = vel + (b1 + const[0])
    res = noisy[...] + STEP_SIZE * vel
    at = lax.broadcasted_iota(jnp.int32, (bins, lanes), 1) - EDGE
    pos = at + tm * frames
    good = (at >= -4) & (at < frames + 4) & (pos >= 0) & (pos < frames * tms)
    mel[...] = res
    mel_in[...] = jnp.where(good, res, 0.0).astype(BF16)


def up_kernel(frames, info, mel, pre_w, pre_b, up_w, up_b, perm, vocal, cols, wide, acc):
    step = pl.program_id(0)
    tm, tms = info[0], info[1]
    taps = pre_w.shape[1]

    @pl.when(step == 0)
    def _():
        melt = mel[...].astype(F32).T
        rows = [melt[4 + q : 4 + q + frames].astype(BF16) for q in range(taps + 2)]
        for s in range(3):
            cols[s * frames : (s + 1) * frames, :] = jnp.concatenate(rows[s : s + taps], axis=1)
        acc[...] = jnp.zeros_like(acc)

    slabs, _, depth, bins = pre_w.shape
    rhs = jnp.concatenate(
        [jnp.concatenate([pre_w[s, k] for k in range(taps)], axis=1) for s in range(slabs)], axis=0
    )
    feats = nt(cols[...], rhs) + pre_b[0]
    line = lax.broadcasted_iota(jnp.int32, (3 * frames, 1), 0)
    pos = tm * frames + line % frames + line // frames - 1
    good = (pos >= 0) & (pos < frames * tms)
    feats = jnp.where(good, feats, 0.0).astype(BF16)
    count, phases, outs = up_w.shape
    for c in range(outs // 128):
        wide[c] = up_w[:, :, c * 128 : (c + 1) * 128].astype(F32).reshape(count * phases, 128)
    for k in range(phases):
        w = [wide.at[c][pl.ds(k, count, stride=phases), :] for c in range(outs // 128)]
        w = jnp.concatenate(w, axis=1).astype(BF16)
        p = (k + 2) % 4
        s = 2 if k < 2 else (1 if k < 6 else 0)
        part = jnp.dot(feats[s * frames : (s + 1) * frames], w, preferred_element_type=F32)
        acc[p * frames : (p + 1) * frames, :] += part

    @pl.when(step == pl.num_programs(0) - 1)
    def _():
        done = (acc[...] + up_b[...]).astype(BF16)
        res = lax.dot_general(done, perm[...], (((0,), (0,)), ((), ())), preferred_element_type=F32)
        vocal[...] = res.astype(BF16)


def exchange(sums):
    devices = lax.axis_size("tm") * lax.axis_size("freq")
    sent = jnp.broadcast_to(sums, (devices, sums.shape[-1]))
    return lax.all_to_all(sent, ("tm", "freq"), 0, 0, tiled=True)


def neighbours(axis):
    n = lax.axis_size(axis)
    up = [(i, i + 1) for i in range(n - 1)]
    return up, [(j, i) for i, j in up]


def shards(
    latent,
    mel_noisy,
    time_shift,
    first_gain,
    first_shift,
    conv_first,
    second_gain,
    second_shift,
    conv_second,
    second_bias,
    out_proj,
    pre_weight,
    pre_bias,
    up_weight,
    up_bias,
):
    chans, bins, frames = latent.shape
    tms, fqs = lax.axis_size("tm"), lax.axis_size("freq")
    tm, fq = lax.axis_index("tm"), lax.axis_index("freq")
    count = float(chans // GROUPS * bins * frames * tms * fqs)
    width = frames + 2 * EDGE
    lanes = -(-width // 128) * 128
    info = jnp.stack([tm, jnp.int32(tms), fq, jnp.int32(fqs)])
    up, down = neighbours("tm")
    x = jnp.transpose(latent, (1, 2, 0))

    if fqs == 2:
        swap = lax.ppermute(jnp.where(fq == 0, x[bins - 2 :], x[:2]), "freq", [(0, 1), (1, 0)])
        top = bottom = swap
    else:
        fup, fdown = neighbours("freq")
        top = lax.ppermute(x[bins - 2 :], "freq", fup)
        bottom = lax.ppermute(x[:2], "freq", fdown)
    last = jnp.concatenate([top[:, frames - EDGE :], x[:, frames - EDGE :], bottom[:, frames - EDGE :]], axis=0)
    first = jnp.concatenate([top[:, :EDGE], x[:, :EDGE], bottom[:, :EDGE]], axis=0)
    left = lax.ppermute(last, "tm", up)
    right = lax.ppermute(first, "tm", down)
    noisy_left = lax.ppermute(mel_noisy[:, frames - EDGE :], "tm", up)
    noisy_right = lax.ppermute(mel_noisy[:, :EDGE], "tm", down)
    noisy = jnp.concatenate(
        [noisy_left, mel_noisy, noisy_right, jnp.zeros((bins, lanes - width), F32)], axis=1
    )

    x32 = x.astype(F32)
    sums = jnp.concatenate([jnp.sum(x32, axis=(0, 1)), jnp.sum(x32 * x32, axis=(0, 1))])[None]
    stats = exchange(sums)

    proj = jnp.stack(split3(out_proj))[:, None, :]
    proj8 = jnp.concatenate([jnp.zeros_like(proj), proj, jnp.zeros((3, 6, chans), BF16)], axis=1).reshape(24, chans)
    rows = 6
    while (bins + 2) % rows:
        rows -= 1
    first_out, moments, base = pl.pallas_call(
        functools.partial(conv_kernel, bins, frames, rows, count),
        out_shape=(
            jax.ShapeDtypeStruct((bins + 2, width, chans), BF16),
            jax.ShapeDtypeStruct((1, 2 * chans), F32),
            jax.ShapeDtypeStruct((bins, 8, width), F32),
        ),
        in_specs=[SMEM] + [VMEM] * 11,
        out_specs=(VMEM,) * 3,
        scratch_shapes=[pltpu.VMEM((bins + 4, width, 3 * chans), BF16)],
        name="conv_first",
    )(
        info, stats, first_gain[None], first_shift[None], time_shift[None], x, left, right, top, bottom,
        conv_first.reshape(9 * chans, chans), proj8,
    )
    stats2 = exchange(moments)

    folded = jnp.einsum("ijco,o->ijc", conv_second.astype(F32), out_proj, precision=lax.Precision.HIGHEST)
    folded = jnp.concatenate([folded, jnp.zeros((3, 5, chans), F32)], axis=1).reshape(24, chans)
    folded = jnp.concatenate(split3(folded), axis=0)
    const = jnp.sum(second_bias * out_proj)[None]
    base = jnp.pad(base.reshape(bins * 8, width), ((0, 0), (0, lanes - width)))
    mel, mel_in = pl.pallas_call(
        functools.partial(mel_kernel, bins, frames, count),
        out_shape=(jax.ShapeDtypeStruct((bins, lanes), F32), jax.ShapeDtypeStruct((bins, lanes), BF16)),
        in_specs=[SMEM, SMEM] + [VMEM] * 7,
        out_specs=(VMEM,) * 2,
        scratch_shapes=[pltpu.VMEM(((bins + 4) * 8, lanes), F32)],
        name="mel",
    )(info, const, stats2, second_gain[None], second_shift[None], first_out, folded, base, noisy)
    mel_next = mel[:, EDGE : EDGE + frames]
    mel_full = lax.all_gather(mel_in, "freq", axis=0, tiled=True)

    taps = pre_weight.shape[1]
    depth = pre_weight.shape[0]
    pieces = lax.all_gather(jnp.transpose(pre_weight, (1, 0, 2)), "tm", axis=0, tiled=False)
    slabs = 1
    while slabs * depth < 384 or tms % slabs:
        slabs += 1
    outs = up_weight.shape[2]
    source = jnp.arange(4 * frames)
    perm = (source[:, None] % frames * 4 + source[:, None] // frames == source[None, :]).astype(BF16)
    vocal = pl.pallas_call(
        functools.partial(up_kernel, frames),
        out_shape=jax.ShapeDtypeStruct((outs, 4 * frames), BF16),
        grid_spec=pltpu.PrefetchScalarGridSpec(
            num_scalar_prefetch=1,
            grid=(tms // slabs,),
            in_specs=[
                pl.BlockSpec((fqs * bins, lanes), lambda i, s: (0, 0)),
                pl.BlockSpec((slabs, taps, depth, fqs * bins), lambda i, s: (i, 0, 0, 0)),
                pl.BlockSpec((1, 1, slabs * depth), lambda i, s: (i, 0, 0)),
                pl.BlockSpec((slabs * depth, up_weight.shape[1], outs), lambda i, s: (i, 0, 0)),
                pl.BlockSpec((1, outs), lambda i, s: (0, 0)),
                pl.BlockSpec((4 * frames, 4 * frames), lambda i, s: (0, 0)),
            ],
            out_specs=pl.BlockSpec((outs, 4 * frames), lambda i, s: (0, 0)),
            scratch_shapes=[
                pltpu.VMEM((3 * frames, taps * fqs * bins), BF16),
                pltpu.VMEM((outs // 128, slabs * depth * up_weight.shape[1], 128), F32),
                pltpu.VMEM((4 * frames, outs), F32),
            ],
        ),
        name="up",
    )(info, mel_full, pieces, pre_bias.reshape(tms // slabs, 1, slabs * depth), up_weight, up_bias[None], perm)
    return (mel_next, vocal)


def solution(mesh):
    in_specs = (
        P(None, "freq", ("song", "tm")),
        P("freq", ("song", "tm")),
        P("song"),
        P(),
        P(),
        P(),
        P(),
        P(),
        P(),
        P(),
        P(),
        P("tm", None, None),
        P(),
        P(None, None, "freq"),
        P("freq"),
    )
    out_specs = (P("freq", ("song", "tm")), P("freq", ("song", "tm")))
    return jax.shard_map(shards, mesh=mesh, in_specs=in_specs, out_specs=out_specs, check_vma=False)
```

```python
import functools

import jax
import jax.numpy as jnp
from jax import lax
from jax.experimental import pallas as pl
from jax.experimental.pallas import tpu as pltpu
from jax.sharding import PartitionSpec as P


GROUPS = 32
EPSILON = 1e-05
STEP_SIZE = 0.25
EDGE = 8
F32 = jnp.float32
BF16 = jnp.bfloat16
VMEM = pl.BlockSpec(memory_space=pltpu.VMEM)
SMEM = pl.BlockSpec(memory_space=pltpu.SMEM)


def nt(a, b):
    return lax.dot_general(a, b, (((1,), (1,)), ((), ())), preferred_element_type=F32)


def split3(x):
    hi = x.astype(BF16)
    rest = x - hi.astype(F32)
    mid = rest.astype(BF16)
    low = (rest - mid.astype(F32)).astype(BF16)
    return hi, mid, low


def norm_terms(stats, gain, shift, count):
    chans = stats.shape[2]
    total = jnp.sum(stats, axis=0)
    if total.shape[0] < 8:
        total = jnp.concatenate([total, jnp.zeros((8 - total.shape[0], chans), F32)], axis=0)
    size = chans // GROUPS
    rows = lax.broadcasted_iota(jnp.int32, (chans, chans), 0) // size
    cols = lax.broadcasted_iota(jnp.int32, (chans, chans), 1) // size
    same = jnp.where(rows == cols, 1.0, 0.0).astype(F32)
    keep = lax.broadcasted_iota(jnp.int32, (8, chans), 0) < 2
    both = jnp.where(keep, total, 0.0)
    groups = lax.dot_general(
        both, same, (((1,), (0,)), ((), ())), precision=lax.Precision.HIGHEST, preferred_element_type=F32
    )
    mean = groups[0:1] / count
    var = groups[1:2] / count - mean * mean
    half = 0.5 * lax.rsqrt(var + EPSILON) * gain
    return half, 0.5 * shift - mean * half


def act_fn(values, scale, shift):
    half = values * scale + shift
    return half + half * jnp.tanh(half)


def edge_flags(axis):
    index = lax.axis_index(axis)
    return (
        jnp.where(index > 0, 1.0, 0.0).astype(F32),
        jnp.where(index < lax.axis_size(axis) - 1, 1.0, 0.0).astype(F32),
    )


def place_rows(rows, begin, chans):
    count, lanes = rows.shape
    rows = jnp.concatenate([rows, jnp.zeros((count, chans - lanes), F32)], axis=1) if lanes < chans else rows
    return jnp.concatenate(
        [jnp.zeros((n, chans), F32) if i != 1 else rows for i, n in enumerate((begin, 0, 8 - begin - count)) if i == 1 or n],
        axis=0,
    )


def sums_kernel(values, noisy, out, last, first):
    rows, frames, chans = values.shape

    def step(r, carry):
        line = values[r]
        last[r] = line[frames - EDGE :]
        first[r] = line[:EDGE]
        x = line.astype(F32).reshape(frames // 8, 8, chans)
        return carry[0] + jnp.sum(x, axis=0), carry[1] + jnp.sum(x * x, axis=0)

    zero = jnp.zeros((8, chans), F32)
    one, two = lax.fori_loop(0, rows, step, (zero, zero), unroll=8)
    both = place_rows(
        jnp.concatenate([jnp.sum(one, axis=0, keepdims=True), jnp.sum(two, axis=0, keepdims=True)], axis=0), 0, chans
    )
    old = noisy[...].T
    to_right = place_rows(old[frames - 4 :], 2, chans)
    to_left = place_rows(old[:4], 2, chans)
    fqs = lax.axis_size("freq")
    me = lax.axis_index("tm") * fqs + lax.axis_index("freq")
    for d in range(out.shape[0]):
        right = jnp.where(me + fqs == d, 1.0, 0.0).astype(F32)
        left = jnp.where(me - fqs == d, 1.0, 0.0).astype(F32)
        out[d] = both + to_right * right + to_left * left


def conv_kernel(bins, frames, rows, count, stats, small, own, left, right, edges,
                weight, out, moments, base, act, made, sems):
    chans = own.shape[-1]
    width = frames + 2 * EDGE
    scale, shift = norm_terms(stats[...], small[0:1], small[1:2], count)
    tshift = small[2:3]
    proj = jnp.concatenate([jnp.broadcast_to(p, (8, chans)) for p in split3(small[5:6])], axis=0)
    has_left, has_right = edge_flags("tm")
    has_top, has_bottom = edge_flags("freq")

    def put(dest, lhs, middle, rhs, bin_ok):
        l32, m32, r32 = lhs.astype(F32), middle.astype(F32), rhs.astype(F32)
        val = jnp.concatenate(
            [
                act_fn(l32, scale, shift) * has_left,
                act_fn(m32, scale, shift),
                act_fn(r32, scale, shift) * has_right,
            ],
            axis=0,
        )
        if bin_ok is not None:
            val = val * bin_ok
        dest[:, 0:chans] = pltpu.roll(val, 1, 0).astype(BF16)
        dest[:, chans : 2 * chans] = val.astype(BF16)
        dest[:, 2 * chans : 3 * chans] = pltpu.roll(val, width - 1, 0).astype(BF16)
        return jnp.concatenate([l32, m32, r32], axis=0).astype(BF16)

    def put_own(dest, i):
        raw = put(dest, left[i], own[i], right[i], None)
        parts = nt(proj, raw)
        base[pl.ds(i, 1), 0:width] = parts[0:1] + parts[8:9] + parts[16:17]

    def put_edge(row, i, flag):
        line = edges[i]
        put(act.at[row], line[:EDGE], line[EDGE : EDGE + frames], line[EDGE + frames :], flag)

    put_edge(0, 0, has_top)
    put_edge(1, 1, has_top)
    for i in range(rows):
        put_own(act.at[i + 2], i)

    blocks = (bins + 2) // rows

    def send(first):
        part = pl.ds(first, rows)
        return pltpu.make_async_copy(made.at[part], out.at[part], sems.at[first // rows])

    def matmul(window, first, acc_s, acc_q):
        lhs = jnp.concatenate([window[i : i + rows] for i in range(3)], axis=-1)
        lhs = lhs.reshape(rows * width, 9 * chans)
        res = jnp.dot(lhs, weight[...], preferred_element_type=F32) + tshift
        res = res.reshape(rows, width, chans).astype(BF16)
        made[pl.ds(first, rows)] = res
        send(first).start()
        for r in range(rows):
            line = first + r
            ok = jnp.where((line >= 1) & (line <= bins), 1.0, 0.0).astype(F32)
            vals = res[r].astype(F32)[EDGE : EDGE + frames] * ok
            vals = vals.reshape(frames // 8, 8, chans)
            acc_s = acc_s + jnp.sum(vals, axis=0)
            acc_q = acc_q + jnp.sum(vals * vals, axis=0)
        return acc_s, acc_q

    def step(b, carry):
        first = b * rows
        window = act.at[pl.ds(first, 2 * rows + 2)]
        for r in range(rows):
            put_own(window.at[rows + 2 + r], jnp.minimum(first + rows + r, bins - 1))
        return matmul(window, first, *carry)

    zero = jnp.zeros((8, chans), F32)
    acc = lax.fori_loop(0, blocks - 1, step, (zero, zero))
    below = edges.shape[0] - 2
    put_edge(bins + 2, below, has_bottom)
    put_edge(bins + 3, below + 1, has_bottom)
    last = (blocks - 1) * rows
    acc_s, acc_q = matmul(act.at[pl.ds(last, rows + 2)], last, *acc)
    both = jnp.concatenate([jnp.sum(acc_s, axis=0, keepdims=True), jnp.sum(acc_q, axis=0, keepdims=True)], axis=0)
    moments[...] = jnp.broadcast_to(both[None], moments.shape)
    for i in range(blocks):
        send(i * rows).wait()


def mel_kernel(bins, frames, count, stats, small, source, folded, base, noisy, borders, mel, mel_in, sums, first_out, sems):
    chans = first_out.shape[-1]
    width = frames + 2 * EDGE
    lanes = sums.shape[1]
    parts = sems.shape[0]
    size = (bins + 2) // parts

    def fetch(i):
        part = pl.ds(i * size, size)
        return pltpu.make_async_copy(source.at[part], first_out.at[part], sems.at[i])

    for i in range(parts):
        fetch(i).start()
    scale, shift = norm_terms(stats[...], small[3:4], small[4:5], count)
    has_left, has_right = edge_flags("tm")
    has_top, has_bottom = edge_flags("freq")
    const = jnp.sum(small[5:6] * small[6:7], axis=1, keepdims=True)
    blank = jnp.zeros((5, chans), F32)
    taps = jnp.concatenate([folded[0], blank, folded[1], blank, folded[2], blank], axis=0)
    weights = jnp.concatenate([p for p in split3(taps)], axis=0)
    sums[...] = jnp.zeros_like(sums)
    group = 256 // width

    def rows(first, flags):
        vals = []
        for q in range(len(flags)):
            val = act_fn(first_out[first + q].astype(F32), scale, shift)
            val = jnp.concatenate(
                [val[:EDGE] * has_left, val[EDGE : EDGE + frames], val[EDGE + frames :] * has_right], axis=0
            )
            vals.append((val if flags[q] is None else val * flags[q]).astype(BF16))
        vals.append(jnp.zeros((256 - width * len(flags), chans), BF16))
        part = nt(weights, jnp.concatenate(vals, axis=0))
        part = part[0:24] + part[24:48] + part[48:72]
        for q in range(len(flags)):
            line = (part if q == 0 else pltpu.roll(part, 256 - q * width, 1))[:, :lanes]
            for i in range(3):
                at = (first + q + 2 - i) * 8
                at = at if isinstance(at, int) else pl.multiple_of(at, 8)
                sums[pl.ds(at, 8), :] += line[8 * i : 8 * i + 8]

    ready = 0
    at = 0
    while at < bins + 2:
        flags = [has_top if q == 0 else has_bottom if q == bins + 1 else None for q in range(at, min(at + group, bins + 2))]
        while ready * size < at + len(flags):
            fetch(ready).wait()
            ready += 1
        rows(at, flags)
        at += len(flags)
    t0 = sums[pl.ds(16, bins, stride=8), :]
    t1 = sums[pl.ds(17, bins, stride=8), :]
    t2 = sums[pl.ds(18, bins, stride=8), :]
    vel = pltpu.roll(t0, 1, 1) + t1 + pltpu.roll(t2, lanes - 1, 1) + base[...] + const

    fqs = lax.axis_size("freq")
    me = lax.axis_index("tm") * fqs + lax.axis_index("freq")
    before = borders[jnp.maximum(me - fqs, 0)][2:6, :bins].T
    behind = borders[jnp.minimum(me + fqs, borders.shape[0] - 1)][2:6, :bins].T
    blank = jnp.zeros((bins, 4), F32)
    old = [blank, before, noisy[...], behind, jnp.zeros((bins, lanes - frames - 12), F32)]
    old = jnp.concatenate(old, axis=1)
    res = old + STEP_SIZE * vel
    at = lax.broadcasted_iota(jnp.int32, (bins, lanes), 1) - EDGE
    pos = at + lax.axis_index("tm") * frames
    good = (at >= -4) & (at < frames + 4) & (pos >= 0) & (pos < frames * lax.axis_size("tm"))
    mel[...] = res[:, EDGE : EDGE + frames]
    mel_in[...] = jnp.where(good, res, 0.0).astype(BF16)


def up_kernel(frames, steps, paired, quarters, *refs):
    mels, refs = (refs[:2], refs[2:]) if paired else (refs[:1], refs[1:])
    pieces, refs = (refs[:4], refs[4:]) if quarters else (refs[:1], refs[1:])
    bias, source, vocal, fetched, wide, sems = refs
    tm, tms = lax.axis_index("tm"), lax.axis_size("tm")
    slabs = tms // steps
    taps = pieces[0].shape[1]
    high = frames + 8
    total, phases, outs = source.shape
    count = total // steps

    def fetch(step):
        return pltpu.make_async_copy(source.at[pl.ds(step * count, count)], fetched.at[step], sems.at[step])

    for step in range(steps):
        fetch(step).start()

    low = lax.axis_index("freq") == 0
    near = lax.axis_index("song") == 0
    if paired:
        a, b = mels[0][...], mels[1][...]
        mel = jnp.concatenate([jnp.where(low, a, b), jnp.where(low, b, a)], axis=0)
    else:
        mel = mels[0][...]
    melt = mel.astype(F32).T
    cols = jnp.concatenate([melt[4 + k : 4 + k + high].astype(BF16) for k in range(taps)], axis=1)
    line = lax.broadcasted_iota(jnp.int32, (high, 1), 0)
    pos = tm * frames + line - 1
    good = (pos >= 0) & (pos < frames * tms)

    def slab(at, k):
        if not quarters:
            return pieces[0][at, k]
        q = [p[at, k] for p in pieces]
        here = [jnp.where(near, q[0], q[1]), jnp.where(near, q[1], q[0])]
        there = [jnp.where(near, q[2], q[3]), jnp.where(near, q[3], q[2])]
        return jnp.concatenate(
            [jnp.where(low, h, t) for h, t in zip(here, there)] + [jnp.where(low, t, h) for h, t in zip(here, there)],
            axis=0,
        )

    shifted = []
    for step in range(steps):
        at = step * count
        rhs = [jnp.concatenate([slab(step * slabs + s, k) for k in range(taps)], axis=1) for s in range(slabs)]
        feats = nt(cols, jnp.concatenate(rhs, axis=0)) + bias[:, at : at + count]
        feats = jnp.where(good, feats, 0.0)
        shifted.append([feats[s : s + frames].astype(BF16) for s in range(3)])
    acc = [jnp.zeros((frames, outs), F32) for _ in range(4)]
    for step in range(steps):
        fetch(step).wait()
        for c in range(outs // 128):
            part = fetched[step, :, :, c * 128 : (c + 1) * 128]
            wide[step, c] = part.astype(F32).reshape(count * phases, 128)
        for k in range(phases):
            p = (k + 2) % 4
            s = 2 if k < 2 else (1 if k < 6 else 0)
            w = [wide.at[step, c][pl.ds(k, count, stride=phases), :] for c in range(outs // 128)]
            w = jnp.concatenate(w, axis=1).astype(BF16)
            acc[p] = acc[p] + jnp.dot(shifted[step][s], w, preferred_element_type=F32)
    size = 4 * frames
    rows = lax.broadcasted_iota(jnp.int32, (size, size), 0)
    place = lax.broadcasted_iota(jnp.int32, (size, size), 1)
    perm = jnp.where(rows % frames * 4 + rows // frames == place, 1.0, 0.0).astype(BF16)
    done = (jnp.concatenate(acc, axis=0) + bias[:, total:]).astype(BF16)
    res = lax.dot_general(done, perm, (((0,), (0,)), ((), ())), preferred_element_type=F32)
    vocal[...] = res.astype(BF16)


def exchange(sums):
    return lax.all_to_all(sums, ("tm", "freq"), 0, 0, tiled=True)


def neighbours(axis):
    n = lax.axis_size(axis)
    up = [(i, i + 1) for i in range(n - 1)]
    return up, [(j, i) for i, j in up]


def after(value, *others):
    return lax.optimization_barrier((value,) + others)[0]


def after(value, *others):
    return lax.optimization_barrier((value,) + others)[0]


def gather_slabs(weight, begin, middle, end):
    tms = lax.axis_size("tm")
    part = weight.shape[1] // 4
    index = lax.axis_index("freq") * 2 + lax.axis_index("song")
    own = after(lax.dynamic_slice_in_dim(weight, index * part, part, axis=1), *begin)
    swap = [(0, 1), (1, 0)]
    own = lax.all_to_all(jnp.broadcast_to(own[None], (tms,) + own.shape), "tm", 0, 0, tiled=True)
    own = after(own, *middle)
    far = lax.ppermute(own, "song", swap)
    other = lax.ppermute(own, "freq", swap)
    other_far = lax.ppermute(after(far, *end), "freq", swap)
    return [own, far, other, other_far]


def shards(
    latent,
    mel_noisy,
    time_shift,
    first_gain,
    first_shift,
    conv_first,
    second_gain,
    second_shift,
    conv_second,
    second_bias,
    out_proj,
    pre_weight,
    pre_bias,
    up_weight,
    up_bias,
):
    chans, bins, frames = latent.shape
    tms, fqs = lax.axis_size("tm"), lax.axis_size("freq")
    fq = lax.axis_index("freq")
    count = float(chans // GROUPS * bins * frames * tms * fqs)
    width = frames + 2 * EDGE
    lanes = -(-width // 128) * 128
    up, down = neighbours("tm")
    swap = [(0, 1), (1, 0)]
    x = jnp.transpose(latent, (1, 2, 0))

    devices = tms * fqs
    payload = jax.ShapeDtypeStruct((devices, 8, chans), F32)
    strip = jax.ShapeDtypeStruct((bins, EDGE, chans), BF16)
    sums, last, first = pl.pallas_call(
        sums_kernel, out_shape=(payload, strip, strip), in_specs=[VMEM] * 2, out_specs=(VMEM,) * 3, name="sums"
    )(x, mel_noisy)
    left = lax.ppermute(last, "tm", up)
    right = lax.ppermute(first, "tm", down)
    stats = exchange(sums)

    if fqs == 2:
        edge = jnp.concatenate([jnp.where(fq == 0, a[bins - 2 : bins], a[:2]) for a in (left, x, right)], axis=1)
        edges = lax.ppermute(edge, "freq", swap)
    else:
        fup, fdown = neighbours("freq")
        low = jnp.concatenate([a[:2] for a in (left, x, right)], axis=1)
        high = jnp.concatenate([a[bins - 2 : bins] for a in (left, x, right)], axis=1)
        edges = jnp.concatenate([lax.ppermute(high, "freq", fup), lax.ppermute(low, "freq", fdown)], axis=0)

    zero = jnp.zeros_like(out_proj)
    small = jnp.stack([first_gain, first_shift, time_shift, second_gain, second_shift, out_proj, second_bias, zero])
    rows = 6
    while (bins + 2) % rows:
        rows -= 1
    first_out, moments, base = pl.pallas_call(
        functools.partial(conv_kernel, bins, frames, rows, count),
        out_shape=(
            jax.ShapeDtypeStruct((bins + 2, width, chans), BF16),
            jax.ShapeDtypeStruct((devices, 2, chans), F32),
            jax.ShapeDtypeStruct((bins, lanes), F32),
        ),
        in_specs=[VMEM] * 7,
        out_specs=(pl.BlockSpec(memory_space=pl.ANY), VMEM, VMEM),
        scratch_shapes=[
            pltpu.VMEM((bins + 4 + rows, width, 3 * chans), BF16),
            pltpu.VMEM((bins + 2, width, chans), BF16),
            pltpu.SemaphoreType.DMA(((bins + 2) // rows,)),
        ],
        name="conv_first",
    )(stats, small, x, left, right, edges, conv_first.reshape(9 * chans, chans))
    stats2 = exchange(moments)

    folded = jnp.einsum("ijco,o->ijc", conv_second.astype(F32), out_proj, precision=lax.Precision.HIGHEST)
    mel_next, mel_in = pl.pallas_call(
        functools.partial(mel_kernel, bins, frames, count),
        out_shape=(jax.ShapeDtypeStruct((bins, frames), F32), jax.ShapeDtypeStruct((bins, lanes), BF16)),
        in_specs=[VMEM] * 2 + [pl.BlockSpec(memory_space=pl.ANY)] + [VMEM] * 4,
        out_specs=(VMEM,) * 2,
        scratch_shapes=[
            pltpu.VMEM(((bins + 4) * 8, lanes), F32),
            pltpu.VMEM((bins + 2, width, chans), BF16),
            pltpu.SemaphoreType.DMA(((bins + 2) // rows,)),
        ],
        name="mel",
    )(stats2, small, first_out, folded, base, mel_noisy, stats)

    depth = pre_weight.shape[0]
    total, phases, outs = up_weight.shape
    weight = jnp.transpose(pre_weight, (1, 0, 2))
    quarters = fqs == 2 and lax.axis_size("song") == 2 and depth % 64 == 0
    if quarters:
        pieces = gather_slabs(weight, (left, right), (moments,), (mel_in,))
    else:
        pieces = [after(lax.all_gather(weight, "tm", axis=0, tiled=False), mel_in)]
    slabs = 1
    while slabs * depth < 384 or tms % slabs:
        slabs += 1
    steps = tms // slabs
    if fqs == 2:
        mels = [mel_in, lax.ppermute(mel_in, "freq", swap)]
    else:
        mels = [lax.all_gather(mel_in, "freq", axis=0, tiled=True)]
    operands = mels + pieces + [jnp.concatenate([pre_bias, up_bias])[None]]
    vocal = pl.pallas_call(
        functools.partial(up_kernel, frames, steps, fqs == 2, quarters),
        out_shape=jax.ShapeDtypeStruct((outs, 4 * frames), BF16),
        in_specs=[VMEM] * len(operands) + [pl.BlockSpec(memory_space=pl.ANY)],
        out_specs=VMEM,
        scratch_shapes=[
            pltpu.VMEM((steps, total // steps, phases, outs), BF16),
            pltpu.VMEM((steps, outs // 128, total // steps * phases, 128), F32),
            pltpu.SemaphoreType.DMA((steps,)),
        ],
        name="up",
    )(*operands, up_weight)
    return (mel_next, vocal)


def solution(mesh):
    in_specs = (
        P(None, "freq", ("song", "tm")),
        P("freq", ("song", "tm")),
        P("song"),
        P(),
        P(),
        P(),
        P(),
        P(),
        P(),
        P(),
        P(),
        P("tm", None, None),
        P(),
        P(None, None, "freq"),
        P("freq"),
    )
    out_specs = (P("freq", ("song", "tm")), P("freq", ("song", "tm")))
    return jax.shard_map(shards, mesh=mesh, in_specs=in_specs, out_specs=out_specs, check_vma=False)
```

```python
import functools

import jax
import jax.numpy as jnp
from jax import lax
from jax.experimental import pallas as pl
from jax.experimental.pallas import tpu as pltpu
from jax.sharding import PartitionSpec as P


GROUPS = 32
EPSILON = 1e-05
STEP_SIZE = 0.25
EDGE = 8
F32 = jnp.float32
BF16 = jnp.bfloat16
VMEM = pl.BlockSpec(memory_space=pltpu.VMEM)
SMEM = pl.BlockSpec(memory_space=pltpu.SMEM)


def nt(a, b):
    return lax.dot_general(a, b, (((1,), (1,)), ((), ())), preferred_element_type=F32)


def split3(x):
    hi = x.astype(BF16)
    rest = x - hi.astype(F32)
    mid = rest.astype(BF16)
    low = (rest - mid.astype(F32)).astype(BF16)
    return hi, mid, low


def norm_terms(stats, gain, shift, count):
    chans = stats.shape[2]
    total = jnp.sum(stats, axis=0)
    if total.shape[0] < 8:
        total = jnp.concatenate([total, jnp.zeros((8 - total.shape[0], chans), F32)], axis=0)
    size = chans // GROUPS
    rows = lax.broadcasted_iota(jnp.int32, (chans, chans), 0) // size
    cols = lax.broadcasted_iota(jnp.int32, (chans, chans), 1) // size
    same = jnp.where(rows == cols, 1.0, 0.0).astype(F32)
    keep = lax.broadcasted_iota(jnp.int32, (8, chans), 0) < 2
    both = jnp.where(keep, total, 0.0)
    groups = lax.dot_general(
        both, same, (((1,), (0,)), ((), ())), precision=lax.Precision.HIGHEST, preferred_element_type=F32
    )
    mean = groups[0:1] / count
    var = groups[1:2] / count - mean * mean
    half = 0.5 * lax.rsqrt(var + EPSILON) * gain
    return half, 0.5 * shift - mean * half


def act_fn(values, scale, shift):
    half = values * scale + shift
    return half + half * jnp.tanh(half)


def edge_flags(axis):
    index = lax.axis_index(axis)
    return (
        jnp.where(index > 0, 1.0, 0.0).astype(F32),
        jnp.where(index < lax.axis_size(axis) - 1, 1.0, 0.0).astype(F32),
    )


def place_rows(rows, begin, chans):
    count, lanes = rows.shape
    rows = jnp.concatenate([rows, jnp.zeros((count, chans - lanes), F32)], axis=1) if lanes < chans else rows
    return jnp.concatenate(
        [jnp.zeros((n, chans), F32) if i != 1 else rows for i, n in enumerate((begin, 0, 8 - begin - count)) if i == 1 or n],
        axis=0,
    )


def sums_kernel(values, noisy, out, last, first):
    rows, frames, chans = values.shape

    def step(r, carry):
        line = values[r]
        last[r] = line[frames - EDGE :]
        first[r] = line[:EDGE]
        x = line.astype(F32).reshape(frames // 8, 8, chans)
        return carry[0] + jnp.sum(x, axis=0), carry[1] + jnp.sum(x * x, axis=0)

    zero = jnp.zeros((8, chans), F32)
    one, two = lax.fori_loop(0, rows, step, (zero, zero), unroll=8)
    both = place_rows(
        jnp.concatenate([jnp.sum(one, axis=0, keepdims=True), jnp.sum(two, axis=0, keepdims=True)], axis=0), 0, chans
    )
    old = noisy[...].T
    to_right = place_rows(old[frames - 4 :], 2, chans)
    to_left = place_rows(old[:4], 2, chans)
    fqs = lax.axis_size("freq")
    me = lax.axis_index("tm") * fqs + lax.axis_index("freq")
    for d in range(out.shape[0]):
        right = jnp.where(me + fqs == d, 1.0, 0.0).astype(F32)
        left = jnp.where(me - fqs == d, 1.0, 0.0).astype(F32)
        out[d] = both + to_right * right + to_left * left


def conv_kernel(bins, frames, rows, count, stats, small, own, left, right, edges,
                weight, out, moments, base, act, made, sems):
    chans = own.shape[-1]
    width = frames + 2 * EDGE
    scale, shift = norm_terms(stats[...], small[0:1], small[1:2], count)
    tshift = small[2:3]
    proj = jnp.concatenate([jnp.broadcast_to(p, (8, chans)) for p in split3(small[5:6])], axis=0)
    has_left, has_right = edge_flags("tm")
    has_top, has_bottom = edge_flags("freq")

    def put(dest, lhs, middle, rhs, bin_ok):
        l32, m32, r32 = lhs.astype(F32), middle.astype(F32), rhs.astype(F32)
        val = jnp.concatenate(
            [
                act_fn(l32, scale, shift) * has_left,
                act_fn(m32, scale, shift),
                act_fn(r32, scale, shift) * has_right,
            ],
            axis=0,
        )
        if bin_ok is not None:
            val = val * bin_ok
        dest[:, 0:chans] = pltpu.roll(val, 1, 0).astype(BF16)
        dest[:, chans : 2 * chans] = val.astype(BF16)
        dest[:, 2 * chans : 3 * chans] = pltpu.roll(val, width - 1, 0).astype(BF16)
        return jnp.concatenate([l32, m32, r32], axis=0).astype(BF16)

    def put_own(dest, i):
        raw = put(dest, left[i], own[i], right[i], None)
        parts = nt(proj, raw)
        base[pl.ds(i, 1), 0:width] = parts[0:1] + parts[8:9] + parts[16:17]

    def put_edge(row, i, flag):
        line = edges[i]
        put(act.at[row], line[:EDGE], line[EDGE : EDGE + frames], line[EDGE + frames :], flag)

    put_edge(0, 0, has_top)
    put_edge(1, 1, has_top)
    for i in range(rows):
        put_own(act.at[i + 2], i)

    blocks = (bins + 2) // rows

    def send(first):
        part = pl.ds(first, rows)
        return pltpu.make_async_copy(made.at[part], out.at[part], sems.at[first // rows])

    def matmul(window, first, acc_s, acc_q):
        lhs = jnp.concatenate([window[i : i + rows] for i in range(3)], axis=-1)
        lhs = lhs.reshape(rows * width, 9 * chans)
        res = jnp.dot(lhs, weight[...], preferred_element_type=F32) + tshift
        res = res.reshape(rows, width, chans).astype(BF16)
        made[pl.ds(first, rows)] = res
        send(first).start()
        for r in range(rows):
            line = first + r
            ok = jnp.where((line >= 1) & (line <= bins), 1.0, 0.0).astype(F32)
            vals = res[r].astype(F32)[EDGE : EDGE + frames] * ok
            vals = vals.reshape(frames // 8, 8, chans)
            acc_s = acc_s + jnp.sum(vals, axis=0)
            acc_q = acc_q + jnp.sum(vals * vals, axis=0)
        return acc_s, acc_q

    def step(b, carry):
        first = b * rows
        window = act.at[pl.ds(first, 2 * rows + 2)]
        for r in range(rows):
            put_own(window.at[rows + 2 + r], jnp.minimum(first + rows + r, bins - 1))
        return matmul(window, first, *carry)

    zero = jnp.zeros((8, chans), F32)
    acc = lax.fori_loop(0, blocks - 1, step, (zero, zero))
    below = edges.shape[0] - 2
    put_edge(bins + 2, below, has_bottom)
    put_edge(bins + 3, below + 1, has_bottom)
    last = (blocks - 1) * rows
    acc_s, acc_q = matmul(act.at[pl.ds(last, rows + 2)], last, *acc)
    both = jnp.concatenate([jnp.sum(acc_s, axis=0, keepdims=True), jnp.sum(acc_q, axis=0, keepdims=True)], axis=0)
    moments[...] = jnp.broadcast_to(both[None], moments.shape)
    for i in range(blocks):
        send(i * rows).wait()


def mel_kernel(bins, frames, count, stats, small, source, folded, base, noisy, borders, mel, mel_in, sums, first_out, sems):
    chans = first_out.shape[-1]
    width = frames + 2 * EDGE
    lanes = sums.shape[1]
    parts = sems.shape[0]
    size = (bins + 2) // parts

    def fetch(i):
        part = pl.ds(i * size, size)
        return pltpu.make_async_copy(source.at[part], first_out.at[part], sems.at[i])

    for i in range(parts):
        fetch(i).start()
    scale, shift = norm_terms(stats[...], small[3:4], small[4:5], count)
    has_left, has_right = edge_flags("tm")
    has_top, has_bottom = edge_flags("freq")
    const = jnp.sum(small[5:6] * small[6:7], axis=1, keepdims=True)
    blank = jnp.zeros((5, chans), F32)
    taps = jnp.concatenate([folded[0], blank, folded[1], blank, folded[2], blank], axis=0)
    weights = jnp.concatenate([p for p in split3(taps)], axis=0)
    sums[...] = jnp.zeros_like(sums)
    group = 256 // width

    def rows(first, flags):
        vals = []
        for q in range(len(flags)):
            val = act_fn(first_out[first + q].astype(F32), scale, shift)
            val = jnp.concatenate(
                [val[:EDGE] * has_left, val[EDGE : EDGE + frames], val[EDGE + frames :] * has_right], axis=0
            )
            vals.append((val if flags[q] is None else val * flags[q]).astype(BF16))
        vals.append(jnp.zeros((256 - width * len(flags), chans), BF16))
        part = nt(weights, jnp.concatenate(vals, axis=0))
        part = part[0:24] + part[24:48] + part[48:72]
        for q in range(len(flags)):
            line = (part if q == 0 else pltpu.roll(part, 256 - q * width, 1))[:, :lanes]
            for i in range(3):
                at = (first + q + 2 - i) * 8
                at = at if isinstance(at, int) else pl.multiple_of(at, 8)
                sums[pl.ds(at, 8), :] += line[8 * i : 8 * i + 8]

    ready = 0
    at = 0
    while at < bins + 2:
        flags = [has_top if q == 0 else has_bottom if q == bins + 1 else None for q in range(at, min(at + group, bins + 2))]
        while ready * size < at + len(flags):
            fetch(ready).wait()
            ready += 1
        rows(at, flags)
        at += len(flags)
    t0 = sums[pl.ds(16, bins, stride=8), :]
    t1 = sums[pl.ds(17, bins, stride=8), :]
    t2 = sums[pl.ds(18, bins, stride=8), :]
    vel = pltpu.roll(t0, 1, 1) + t1 + pltpu.roll(t2, lanes - 1, 1) + base[...] + const

    fqs = lax.axis_size("freq")
    me = lax.axis_index("tm") * fqs + lax.axis_index("freq")
    before = borders[jnp.maximum(me - fqs, 0)][2:6, :bins].T
    behind = borders[jnp.minimum(me + fqs, borders.shape[0] - 1)][2:6, :bins].T
    blank = jnp.zeros((bins, 4), F32)
    old = [blank, before, noisy[...], behind, jnp.zeros((bins, lanes - frames - 12), F32)]
    old = jnp.concatenate(old, axis=1)
    res = old + STEP_SIZE * vel
    at = lax.broadcasted_iota(jnp.int32, (bins, lanes), 1) - EDGE
    pos = at + lax.axis_index("tm") * frames
    good = (at >= -4) & (at < frames + 4) & (pos >= 0) & (pos < frames * lax.axis_size("tm"))
    mel[...] = res[:, EDGE : EDGE + frames]
    mel_in[...] = jnp.where(good, res, 0.0).astype(BF16)


def up_kernel(frames, steps, paired, quarters, *refs):
    mels, refs = (refs[:2], refs[2:]) if paired else (refs[:1], refs[1:])
    pieces, refs = (refs[:4], refs[4:]) if quarters else (refs[:1], refs[1:])
    bias, final, source, vocal, fetched, wide, sems = refs
    tm, tms = lax.axis_index("tm"), lax.axis_size("tm")
    slabs, taps, depth, _ = pieces[0].shape
    high = frames + 8
    total, phases, outs = source.shape
    steps = 4 if quarters else steps
    count = total // steps
    fq, song = lax.axis_index("freq"), lax.axis_index("song")
    places = [fq * 2 + song, fq * 2 + 1 - song, 2 - fq * 2 + song, 3 - fq * 2 - song] if quarters else None

    def fetch(step):
        if not quarters:
            at = pl.ds(step * count, count)
            return [pltpu.make_async_copy(source.at[at], fetched.at[step], sems.at[step, 0])]
        return [
            pltpu.make_async_copy(
                source.at[pl.ds(s * 4 * depth + places[step] * depth, depth)],
                fetched.at[step, pl.ds(s * depth, depth)],
                sems.at[step, s],
            )
            for s in range(slabs)
        ]

    for step in range(steps):
        for copy in fetch(step):
            copy.start()

    if paired:
        a, b = mels[0][...], mels[1][...]
        mel = jnp.concatenate([jnp.where(fq == 0, a, b), jnp.where(fq == 0, b, a)], axis=0)
    else:
        mel = mels[0][...]
    melt = mel.astype(F32).T
    cols = jnp.concatenate([melt[4 + k : 4 + k + high].astype(BF16) for k in range(taps)], axis=1)
    line = lax.broadcasted_iota(jnp.int32, (high, 1), 0)
    pos = tm * frames + line - 1
    good = (pos >= 0) & (pos < frames * tms)

    shifted = []
    for step in range(steps):
        piece, per = (pieces[step], range(slabs)) if quarters else (pieces[0], range(step * slabs // steps, (step + 1) * slabs // steps))
        rhs = [jnp.concatenate([piece[s, k] for k in range(taps)], axis=1) for s in per]
        feats = nt(cols, jnp.concatenate(rhs, axis=0)) + bias[places[step] if quarters else step]
        feats = jnp.where(good, feats, 0.0)
        shifted.append([feats[s : s + frames].astype(BF16) for s in range(3)])
    acc = [jnp.zeros((frames, outs), F32) for _ in range(4)]
    for step in range(steps):
        for copy in fetch(step):
            copy.wait()
        for c in range(outs // 128):
            part = fetched[step, :, :, c * 128 : (c + 1) * 128]
            wide[step, c] = part.astype(F32).reshape(count * phases, 128)
        for k in range(phases):
            p = (k + 2) % 4
            s = 2 if k < 2 else (1 if k < 6 else 0)
            w = [wide.at[step, c][pl.ds(k, count, stride=phases), :] for c in range(outs // 128)]
            w = jnp.concatenate(w, axis=1).astype(BF16)
            acc[p] = acc[p] + jnp.dot(shifted[step][s], w, preferred_element_type=F32)
    size = 4 * frames
    rows = lax.broadcasted_iota(jnp.int32, (size, size), 0)
    place = lax.broadcasted_iota(jnp.int32, (size, size), 1)
    perm = jnp.where(rows % frames * 4 + rows // frames == place, 1.0, 0.0).astype(BF16)
    done = (jnp.concatenate(acc, axis=0) + final[...]).astype(BF16)
    res = lax.dot_general(done, perm, (((0,), (0,)), ((), ())), preferred_element_type=F32)
    vocal[...] = res.astype(BF16)


def exchange(sums):
    return lax.all_to_all(sums, ("tm", "freq"), 0, 0, tiled=True)


def neighbours(axis):
    n = lax.axis_size(axis)
    up = [(i, i + 1) for i in range(n - 1)]
    return up, [(j, i) for i, j in up]


def after(value, *others):
    return lax.optimization_barrier((value,) + others)[0]


def after(value, *others):
    return lax.optimization_barrier((value,) + others)[0]


def gather_slabs(weight, begin, middle, end):
    tms = lax.axis_size("tm")
    part = weight.shape[1] // 4
    index = lax.axis_index("freq") * 2 + lax.axis_index("song")
    own = after(lax.dynamic_slice_in_dim(weight, index * part, part, axis=1), *begin)
    swap = [(0, 1), (1, 0)]
    own = lax.all_to_all(jnp.broadcast_to(own[None], (tms,) + own.shape), "tm", 0, 0, tiled=True)
    own = after(own, *middle)
    far = lax.ppermute(own, "song", swap)
    other = lax.ppermute(own, "freq", swap)
    other_far = lax.ppermute(after(far, *end), "freq", swap)
    return [own, far, other, other_far]


def shards(
    latent,
    mel_noisy,
    time_shift,
    first_gain,
    first_shift,
    conv_first,
    second_gain,
    second_shift,
    conv_second,
    second_bias,
    out_proj,
    pre_weight,
    pre_bias,
    up_weight,
    up_bias,
):
    chans, bins, frames = latent.shape
    tms, fqs = lax.axis_size("tm"), lax.axis_size("freq")
    fq = lax.axis_index("freq")
    count = float(chans // GROUPS * bins * frames * tms * fqs)
    width = frames + 2 * EDGE
    lanes = -(-width // 128) * 128
    up, down = neighbours("tm")
    swap = [(0, 1), (1, 0)]
    x = jnp.transpose(latent, (1, 2, 0))

    devices = tms * fqs
    payload = jax.ShapeDtypeStruct((devices, 8, chans), F32)
    strip = jax.ShapeDtypeStruct((bins, EDGE, chans), BF16)
    sums, last, first = pl.pallas_call(
        sums_kernel, out_shape=(payload, strip, strip), in_specs=[VMEM] * 2, out_specs=(VMEM,) * 3, name="sums"
    )(x, mel_noisy)
    left = lax.ppermute(last, "tm", up)
    right = lax.ppermute(first, "tm", down)
    stats = exchange(sums)

    if fqs == 2:
        edge = jnp.concatenate([jnp.where(fq == 0, a[bins - 2 : bins], a[:2]) for a in (left, x, right)], axis=1)
        edges = lax.ppermute(edge, "freq", swap)
    else:
        fup, fdown = neighbours("freq")
        low = jnp.concatenate([a[:2] for a in (left, x, right)], axis=1)
        high = jnp.concatenate([a[bins - 2 : bins] for a in (left, x, right)], axis=1)
        edges = jnp.concatenate([lax.ppermute(high, "freq", fup), lax.ppermute(low, "freq", fdown)], axis=0)

    zero = jnp.zeros_like(out_proj)
    small = jnp.stack([first_gain, first_shift, time_shift, second_gain, second_shift, out_proj, second_bias, zero])
    rows = 11
    while (bins + 2) % rows:
        rows -= 1
    first_out, moments, base = pl.pallas_call(
        functools.partial(conv_kernel, bins, frames, rows, count),
        out_shape=(
            jax.ShapeDtypeStruct((bins + 2, width, chans), BF16),
            jax.ShapeDtypeStruct((devices, 2, chans), F32),
            jax.ShapeDtypeStruct((bins, lanes), F32),
        ),
        in_specs=[VMEM] * 7,
        out_specs=(pl.BlockSpec(memory_space=pl.ANY), VMEM, VMEM),
        scratch_shapes=[
            pltpu.VMEM((bins + 4 + rows, width, 3 * chans), BF16),
            pltpu.VMEM((bins + 2, width, chans), BF16),
            pltpu.SemaphoreType.DMA(((bins + 2) // rows,)),
        ],
        name="conv_first",
    )(stats, small, x, left, right, edges, conv_first.reshape(9 * chans, chans))
    stats2 = exchange(moments)

    parts = 2
    while (bins + 2) % parts:
        parts -= 1
    folded = jnp.einsum("ijco,o->ijc", conv_second.astype(F32), out_proj, precision=lax.Precision.HIGHEST)
    mel_next, mel_in = pl.pallas_call(
        functools.partial(mel_kernel, bins, frames, count),
        out_shape=(jax.ShapeDtypeStruct((bins, frames), F32), jax.ShapeDtypeStruct((bins, lanes), BF16)),
        in_specs=[VMEM] * 2 + [pl.BlockSpec(memory_space=pl.ANY)] + [VMEM] * 4,
        out_specs=(VMEM,) * 2,
        scratch_shapes=[
            pltpu.VMEM(((bins + 4) * 8, lanes), F32),
            pltpu.VMEM((bins + 2, width, chans), BF16),
            pltpu.SemaphoreType.DMA((parts,)),
        ],
        name="mel",
    )(stats2, small, first_out, folded, base, mel_noisy, stats)

    depth = pre_weight.shape[0]
    total, phases, outs = up_weight.shape
    weight = jnp.transpose(pre_weight, (1, 0, 2))
    quarters = fqs == 2 and lax.axis_size("song") == 2 and depth % 64 == 0
    if quarters:
        pieces = gather_slabs(weight, (right,), (moments,), (mel_in,))
    else:
        pieces = [after(lax.all_gather(weight, "tm", axis=0, tiled=False), mel_in)]
    slabs = 1
    while slabs * depth < 384 or tms % slabs:
        slabs += 1
    steps = tms // slabs
    if fqs == 2:
        mels = [mel_in, lax.ppermute(mel_in, "freq", swap)]
    else:
        mels = [lax.all_gather(mel_in, "freq", axis=0, tiled=True)]
    if quarters:
        steps = 4
        bias = pre_bias.reshape(tms, 4, depth // 4).swapaxes(0, 1).reshape(4, 1, total // 4)
    else:
        bias = pre_bias.reshape(steps, 1, total // steps)
    operands = mels + pieces + [bias, up_bias[None]]
    vocal = pl.pallas_call(
        functools.partial(up_kernel, frames, steps, fqs == 2, quarters),
        out_shape=jax.ShapeDtypeStruct((outs, 4 * frames), BF16),
        in_specs=[VMEM] * len(operands) + [pl.BlockSpec(memory_space=pl.ANY)],
        out_specs=VMEM,
        scratch_shapes=[
            pltpu.VMEM((steps, total // steps, phases, outs), BF16),
            pltpu.VMEM((steps, outs // 128, total // steps * phases, 128), F32),
            pltpu.SemaphoreType.DMA((steps, tms if quarters else 1)),
        ],
        name="up",
    )(*operands, up_weight)
    return (mel_next, vocal)


def solution(mesh):
    in_specs = (
        P(None, "freq", ("song", "tm")),
        P("freq", ("song", "tm")),
        P("song"),
        P(),
        P(),
        P(),
        P(),
        P(),
        P(),
        P(),
        P(),
        P("tm", None, None),
        P(),
        P(None, None, "freq"),
        P("freq"),
    )
    out_specs = (P("freq", ("song", "tm")), P("freq", ("song", "tm")))
    return jax.shard_map(shards, mesh=mesh, in_specs=in_specs, out_specs=out_specs, check_vma=False)
```

```python
import functools

import jax
import jax.numpy as jnp
from jax import lax
from jax.experimental import pallas as pl
from jax.experimental.pallas import tpu as pltpu
from jax.sharding import PartitionSpec as P


GROUPS = 32
EPSILON = 1e-05
STEP_SIZE = 0.25
EDGE = 8
READY = 1
F32 = jnp.float32
BF16 = jnp.bfloat16
VMEM = pl.BlockSpec(memory_space=pltpu.VMEM)
SMEM = pl.BlockSpec(memory_space=pltpu.SMEM)


def nt(a, b):
    return lax.dot_general(a, b, (((1,), (1,)), ((), ())), preferred_element_type=F32)


def split3(x):
    hi = x.astype(BF16)
    rest = x - hi.astype(F32)
    mid = rest.astype(BF16)
    low = (rest - mid.astype(F32)).astype(BF16)
    return hi, mid, low


def norm_terms(stats, gain, shift, count):
    chans = stats.shape[2]
    total = jnp.sum(stats, axis=0)
    if total.shape[0] < 8:
        total = jnp.concatenate([total, jnp.zeros((8 - total.shape[0], chans), F32)], axis=0)
    size = chans // GROUPS
    rows = lax.broadcasted_iota(jnp.int32, (chans, chans), 0) // size
    cols = lax.broadcasted_iota(jnp.int32, (chans, chans), 1) // size
    same = jnp.where(rows == cols, 1.0, 0.0).astype(F32)
    keep = lax.broadcasted_iota(jnp.int32, (8, chans), 0) < 2
    both = jnp.where(keep, total, 0.0)
    groups = lax.dot_general(
        both, same, (((1,), (0,)), ((), ())), precision=lax.Precision.HIGHEST, preferred_element_type=F32
    )
    mean = groups[0:1] / count
    var = groups[1:2] / count - mean * mean
    half = 0.5 * lax.rsqrt(var + EPSILON) * gain
    return half, 0.5 * shift - mean * half


def act_fn(values, scale, shift):
    half = values * scale + shift
    return half + half * jnp.tanh(half)


def edge_flags(axis):
    index = lax.axis_index(axis)
    return (
        jnp.where(index > 0, 1.0, 0.0).astype(F32),
        jnp.where(index < lax.axis_size(axis) - 1, 1.0, 0.0).astype(F32),
    )


def place_rows(rows, begin, chans):
    count, lanes = rows.shape
    rows = jnp.concatenate([rows, jnp.zeros((count, chans - lanes), F32)], axis=1) if lanes < chans else rows
    return jnp.concatenate(
        [jnp.zeros((n, chans), F32) if i != 1 else rows for i, n in enumerate((begin, 0, 8 - begin - count)) if i == 1 or n],
        axis=0,
    )


def sums_kernel(values, noisy, out, last, first):
    rows, frames, chans = values.shape

    def step(r, carry):
        line = values[r]
        last[r] = line[frames - EDGE :]
        first[r] = line[:EDGE]
        x = line.astype(F32).reshape(frames // 8, 8, chans)
        return carry[0] + jnp.sum(x, axis=0), carry[1] + jnp.sum(x * x, axis=0)

    zero = jnp.zeros((8, chans), F32)
    one, two = lax.fori_loop(0, rows, step, (zero, zero), unroll=8)
    both = place_rows(
        jnp.concatenate([jnp.sum(one, axis=0, keepdims=True), jnp.sum(two, axis=0, keepdims=True)], axis=0), 0, chans
    )
    old = noisy[...].T
    to_right = place_rows(old[frames - 4 :], 2, chans)
    to_left = place_rows(old[:4], 2, chans)
    fqs = lax.axis_size("freq")
    me = lax.axis_index("tm") * fqs + lax.axis_index("freq")
    for d in range(out.shape[0]):
        right = jnp.where(me + fqs == d, 1.0, 0.0).astype(F32)
        left = jnp.where(me - fqs == d, 1.0, 0.0).astype(F32)
        out[d] = both + to_right * right + to_left * left


def conv_kernel(bins, frames, rows, count, stats, small, own, left, right, edges,
                weight, out, moments, base, act, made, sems):
    chans = own.shape[-1]
    width = frames + 2 * EDGE
    scale, shift = norm_terms(stats[...], small[0:1], small[1:2], count)
    tshift = small[2:3]
    proj = jnp.concatenate([jnp.broadcast_to(p, (8, chans)) for p in split3(small[5:6])], axis=0)
    has_left, has_right = edge_flags("tm")
    has_top, has_bottom = edge_flags("freq")

    def put(dest, lhs, middle, rhs, bin_ok):
        l32, m32, r32 = lhs.astype(F32), middle.astype(F32), rhs.astype(F32)
        val = jnp.concatenate(
            [
                act_fn(l32, scale, shift) * has_left,
                act_fn(m32, scale, shift),
                act_fn(r32, scale, shift) * has_right,
            ],
            axis=0,
        )
        if bin_ok is not None:
            val = val * bin_ok
        dest[:, 0:chans] = pltpu.roll(val, 1, 0).astype(BF16)
        dest[:, chans : 2 * chans] = val.astype(BF16)
        dest[:, 2 * chans : 3 * chans] = pltpu.roll(val, width - 1, 0).astype(BF16)
        return jnp.concatenate([l32, m32, r32], axis=0).astype(BF16)

    def put_own(dest, i):
        raw = put(dest, left[i], own[i], right[i], None)
        parts = nt(proj, raw)
        base[pl.ds(i, 1), 0:width] = parts[0:1] + parts[8:9] + parts[16:17]

    def put_edge(row, i, flag):
        line = edges[i]
        put(act.at[row], line[:EDGE], line[EDGE : EDGE + frames], line[EDGE + frames :], flag)

    put_edge(0, 0, has_top)
    put_edge(1, 1, has_top)
    for i in range(rows):
        put_own(act.at[i + 2], i)

    blocks = (bins + 2) // rows

    def send(first):
        part = pl.ds(first, rows)
        return pltpu.make_async_copy(made.at[part], out.at[part], sems.at[first // rows])

    def matmul(window, first, acc_s, acc_q):
        lhs = jnp.concatenate([window[i : i + rows] for i in range(3)], axis=-1)
        lhs = lhs.reshape(rows * width, 9 * chans)
        res = jnp.dot(lhs, weight[...], preferred_element_type=F32) + tshift
        res = res.reshape(rows, width, chans).astype(BF16)
        made[pl.ds(first, rows)] = res
        send(first).start()
        for r in range(rows):
            line = first + r
            ok = jnp.where((line >= 1) & (line <= bins), 1.0, 0.0).astype(F32)
            vals = res[r].astype(F32)[EDGE : EDGE + frames] * ok
            vals = vals.reshape(frames // 8, 8, chans)
            acc_s = acc_s + jnp.sum(vals, axis=0)
            acc_q = acc_q + jnp.sum(vals * vals, axis=0)
        return acc_s, acc_q

    def step(b, carry):
        first = b * rows
        window = act.at[pl.ds(first, 2 * rows + 2)]
        for r in range(rows):
            put_own(window.at[rows + 2 + r], jnp.minimum(first + rows + r, bins - 1))
        return matmul(window, first, *carry)

    zero = jnp.zeros((8, chans), F32)
    acc = lax.fori_loop(0, blocks - 1, step, (zero, zero))
    below = edges.shape[0] - 2
    put_edge(bins + 2, below, has_bottom)
    put_edge(bins + 3, below + 1, has_bottom)
    last = (blocks - 1) * rows
    acc_s, acc_q = matmul(act.at[pl.ds(last, rows + 2)], last, *acc)
    both = jnp.concatenate([jnp.sum(acc_s, axis=0, keepdims=True), jnp.sum(acc_q, axis=0, keepdims=True)], axis=0)
    moments[...] = jnp.broadcast_to(both[None], moments.shape)
    for i in range(blocks):
        send(i * rows).wait()


def mel_kernel(bins, frames, count, stats, small, source, folded, base, noisy, borders, mel, mel_in, sums, first_out, sems):
    chans = first_out.shape[-1]
    width = frames + 2 * EDGE
    lanes = sums.shape[1]
    parts = sems.shape[0]
    size = (bins + 2) // parts

    def fetch(i):
        part = pl.ds(i * size, size)
        return pltpu.make_async_copy(source.at[part], first_out.at[part], sems.at[i])

    for i in range(parts):
        fetch(i).start()
    scale, shift = norm_terms(stats[...], small[3:4], small[4:5], count)
    has_left, has_right = edge_flags("tm")
    has_top, has_bottom = edge_flags("freq")
    const = jnp.sum(small[5:6] * small[6:7], axis=1, keepdims=True)
    blank = jnp.zeros((5, chans), F32)
    taps = jnp.concatenate([folded[0], blank, folded[1], blank, folded[2], blank], axis=0)
    weights = jnp.concatenate([p for p in split3(taps)], axis=0)
    sums[...] = jnp.zeros_like(sums)
    group = 256 // width

    def rows(first, flags):
        vals = []
        for q in range(len(flags)):
            val = act_fn(first_out[first + q].astype(F32), scale, shift)
            val = jnp.concatenate(
                [val[:EDGE] * has_left, val[EDGE : EDGE + frames], val[EDGE + frames :] * has_right], axis=0
            )
            vals.append((val if flags[q] is None else val * flags[q]).astype(BF16))
        vals.append(jnp.zeros((256 - width * len(flags), chans), BF16))
        part = nt(weights, jnp.concatenate(vals, axis=0))
        part = part[0:24] + part[24:48] + part[48:72]
        for q in range(len(flags)):
            line = (part if q == 0 else pltpu.roll(part, 256 - q * width, 1))[:, :lanes]
            for i in range(3):
                at = (first + q + 2 - i) * 8
                at = at if isinstance(at, int) else pl.multiple_of(at, 8)
                sums[pl.ds(at, 8), :] += line[8 * i : 8 * i + 8]

    ready = 0
    at = 0
    while at < bins + 2:
        flags = [has_top if q == 0 else has_bottom if q == bins + 1 else None for q in range(at, min(at + group, bins + 2))]
        while ready * size < at + len(flags):
            fetch(ready).wait()
            ready += 1
        rows(at, flags)
        at += len(flags)
    t0 = sums[pl.ds(16, bins, stride=8), :]
    t1 = sums[pl.ds(17, bins, stride=8), :]
    t2 = sums[pl.ds(18, bins, stride=8), :]
    vel = pltpu.roll(t0, 1, 1) + t1 + pltpu.roll(t2, lanes - 1, 1) + base[...] + const

    fqs = lax.axis_size("freq")
    me = lax.axis_index("tm") * fqs + lax.axis_index("freq")
    before = borders[jnp.maximum(me - fqs, 0)][2:6, :bins].T
    behind = borders[jnp.minimum(me + fqs, borders.shape[0] - 1)][2:6, :bins].T
    blank = jnp.zeros((bins, 4), F32)
    old = [blank, before, noisy[...], behind, jnp.zeros((bins, lanes - frames - 12), F32)]
    old = jnp.concatenate(old, axis=1)
    res = old + STEP_SIZE * vel
    at = lax.broadcasted_iota(jnp.int32, (bins, lanes), 1) - EDGE
    pos = at + lax.axis_index("tm") * frames
    good = (at >= -4) & (at < frames + 4) & (pos >= 0) & (pos < frames * lax.axis_size("tm"))
    mel[...] = res[:, EDGE : EDGE + frames]
    mel_in[...] = jnp.where(good, res, 0.0).astype(BF16)


def piece_places():
    fq, song = lax.axis_index("freq"), lax.axis_index("song")
    return [fq * 2 + song, fq * 2 + 1 - song, 2 - fq * 2 + song, 3 - fq * 2 - song]


def piece_rows(source, target, sems, place, slabs):
    depth = source.shape[0] // slabs // 4
    return [
        pltpu.make_async_copy(
            source.at[pl.ds((s * 4 + place) * depth, depth)], target.at[pl.ds(s * depth, depth)], sems.at[s]
        )
        for s in range(slabs)
    ]


def taps_kernel(which, slabs, source, out, fetched, wide, sems):
    copies = piece_rows(source, fetched, sems, piece_places()[which], slabs)
    count, phases, outs = fetched.shape
    for copy in copies:
        copy.start()
    for copy in copies:
        copy.wait()
    for c in range(outs // 128):
        cols = slice(c * 128, (c + 1) * 128)
        wide[c] = fetched[:, :, cols].astype(F32).reshape(count * phases, 128)
        for k in range(phases):
            out[k, :, cols] = wide.at[c][pl.ds(k, count, stride=phases), :].astype(BF16)


def split_taps(weight, which, slabs):
    total, phases, outs = weight.shape
    count = total // 4
    return pl.pallas_call(
        functools.partial(taps_kernel, which, slabs),
        out_shape=jax.ShapeDtypeStruct((phases, count, outs), BF16),
        in_specs=[pl.BlockSpec(memory_space=pl.ANY)],
        out_specs=VMEM,
        scratch_shapes=[
            pltpu.VMEM((count, phases, outs), BF16),
            pltpu.VMEM((outs // 128, count * phases, 128), F32),
            pltpu.SemaphoreType.DMA((slabs,)),
        ],
        name="taps",
    )(weight)


def up_kernel(frames, steps, paired, quarters, *refs):
    mels, refs = (refs[:2], refs[2:]) if paired else (refs[:1], refs[1:])
    pieces, refs = (refs[:4], refs[4:]) if quarters else (refs[:1], refs[1:])
    bias, final, source, *refs = refs
    ready, (vocal, fetched, wide, split, sems) = refs[:-5], refs[-5:]
    tm, tms = lax.axis_index("tm"), lax.axis_size("tm")
    slabs, taps, _, _ = pieces[0].shape
    high = frames + 8
    total, phases, outs = source.shape
    steps = 4 if quarters else steps
    count = total // steps
    fq = lax.axis_index("freq")
    places = piece_places() if quarters else None

    def fetch(step):
        if step < len(ready):
            return [pltpu.make_async_copy(ready[step], split.at[step], sems.at[step, 0])]
        if not quarters:
            at = pl.ds(step * count, count)
            return [pltpu.make_async_copy(source.at[at], fetched.at[step], sems.at[step, 0])]
        return piece_rows(source, fetched.at[step - len(ready)], sems.at[step], places[step], slabs)

    for step in range(steps):
        for copy in fetch(step):
            copy.start()

    if paired:
        a, b = mels[0][...], mels[1][...]
        mel = jnp.concatenate([jnp.where(fq == 0, a, b), jnp.where(fq == 0, b, a)], axis=0)
    else:
        mel = mels[0][...]
    melt = mel.astype(F32).T
    cols = jnp.concatenate([melt[4 + k : 4 + k + high].astype(BF16) for k in range(taps)], axis=1)
    line = lax.broadcasted_iota(jnp.int32, (high, 1), 0)
    pos = tm * frames + line - 1
    good = (pos >= 0) & (pos < frames * tms)

    shifted = []
    for step in range(steps):
        piece, per = (pieces[step], range(slabs)) if quarters else (pieces[0], range(step * slabs // steps, (step + 1) * slabs // steps))
        rhs = [jnp.concatenate([piece[s, k] for k in range(taps)], axis=1) for s in per]
        feats = nt(cols, jnp.concatenate(rhs, axis=0)) + bias[places[step] if quarters else step]
        feats = jnp.where(good, feats, 0.0)
        shifted.append([feats[s : s + frames].astype(BF16) for s in range(3)])
    acc = [jnp.zeros((frames, outs), F32) for _ in range(4)]
    for step in range(steps):
        for copy in fetch(step):
            copy.wait()
        if step >= len(ready):
            at = step - len(ready)
            for c in range(outs // 128):
                part = fetched[at, :, :, c * 128 : (c + 1) * 128]
                wide[at, c] = part.astype(F32).reshape(count * phases, 128)
        for k in range(phases):
            p = (k + 2) % 4
            s = 2 if k < 2 else (1 if k < 6 else 0)
            if step < len(ready):
                w = split[step, k]
            else:
                w = [wide.at[at, c][pl.ds(k, count, stride=phases), :] for c in range(outs // 128)]
                w = jnp.concatenate(w, axis=1).astype(BF16)
            acc[p] = acc[p] + jnp.dot(shifted[step][s], w, preferred_element_type=F32)
    size = 4 * frames
    rows = lax.broadcasted_iota(jnp.int32, (size, size), 0)
    place = lax.broadcasted_iota(jnp.int32, (size, size), 1)
    perm = jnp.where(rows % frames * 4 + rows // frames == place, 1.0, 0.0).astype(BF16)
    done = (jnp.concatenate(acc, axis=0) + final[...]).astype(BF16)
    res = lax.dot_general(done, perm, (((0,), (0,)), ((), ())), preferred_element_type=F32)
    vocal[...] = res.astype(BF16)


def exchange(sums):
    return lax.all_to_all(sums, ("tm", "freq"), 0, 0, tiled=True)


def neighbours(axis):
    n = lax.axis_size(axis)
    up = [(i, i + 1) for i in range(n - 1)]
    return up, [(j, i) for i, j in up]


def after(value, *others):
    return lax.optimization_barrier((value,) + others)[0]


def after(value, *others):
    return lax.optimization_barrier((value,) + others)[0]


def gather_slabs(weight, begin, middle, end):
    tms = lax.axis_size("tm")
    part = weight.shape[1] // 4
    index = lax.axis_index("freq") * 2 + lax.axis_index("song")
    own = lax.dynamic_slice_in_dim(weight, index * part, part, axis=1)
    swap = [(0, 1), (1, 0)]
    own = jnp.broadcast_to(own[None], (tms,) + own.shape)
    own = lax.all_to_all(after(own, *begin), "tm", 0, 0, tiled=True)
    own = after(own, *middle)
    far = lax.ppermute(own, "song", swap)
    other = lax.ppermute(own, "freq", swap)
    other_far = lax.ppermute(after(far, *end), "freq", swap)
    return [own, far, other, other_far]


def shards(
    latent,
    mel_noisy,
    time_shift,
    first_gain,
    first_shift,
    conv_first,
    second_gain,
    second_shift,
    conv_second,
    second_bias,
    out_proj,
    pre_weight,
    pre_bias,
    up_weight,
    up_bias,
):
    chans, bins, frames = latent.shape
    tms, fqs = lax.axis_size("tm"), lax.axis_size("freq")
    fq = lax.axis_index("freq")
    count = float(chans // GROUPS * bins * frames * tms * fqs)
    width = frames + 2 * EDGE
    lanes = -(-width // 128) * 128
    up, down = neighbours("tm")
    swap = [(0, 1), (1, 0)]
    x = jnp.transpose(latent, (1, 2, 0))

    devices = tms * fqs
    payload = jax.ShapeDtypeStruct((devices, 8, chans), F32)
    strip = jax.ShapeDtypeStruct((bins, EDGE, chans), BF16)
    sums, last, first = pl.pallas_call(
        sums_kernel, out_shape=(payload, strip, strip), in_specs=[VMEM] * 2, out_specs=(VMEM,) * 3, name="sums"
    )(x, mel_noisy)
    left = lax.ppermute(last, "tm", up)
    right = lax.ppermute(first, "tm", down)
    stats = exchange(sums)

    if fqs == 2:
        edge = jnp.concatenate([jnp.where(fq == 0, a[bins - 2 : bins], a[:2]) for a in (left, x, right)], axis=1)
        edges = lax.ppermute(edge, "freq", swap)
    else:
        fup, fdown = neighbours("freq")
        low = jnp.concatenate([a[:2] for a in (left, x, right)], axis=1)
        high = jnp.concatenate([a[bins - 2 : bins] for a in (left, x, right)], axis=1)
        edges = jnp.concatenate([lax.ppermute(high, "freq", fup), lax.ppermute(low, "freq", fdown)], axis=0)

    zero = jnp.zeros_like(out_proj)
    small = jnp.stack([first_gain, first_shift, time_shift, second_gain, second_shift, out_proj, second_bias, zero])
    rows = 11
    while (bins + 2) % rows:
        rows -= 1
    first_out, moments, base = pl.pallas_call(
        functools.partial(conv_kernel, bins, frames, rows, count),
        out_shape=(
            jax.ShapeDtypeStruct((bins + 2, width, chans), BF16),
            jax.ShapeDtypeStruct((devices, 2, chans), F32),
            jax.ShapeDtypeStruct((bins, lanes), F32),
        ),
        in_specs=[VMEM] * 7,
        out_specs=(pl.BlockSpec(memory_space=pl.ANY), VMEM, VMEM),
        scratch_shapes=[
            pltpu.VMEM((bins + 4 + rows, width, 3 * chans), BF16),
            pltpu.VMEM((bins + 2, width, chans), BF16),
            pltpu.SemaphoreType.DMA(((bins + 2) // rows,)),
        ],
        name="conv_first",
    )(stats, small, x, left, right, edges, conv_first.reshape(9 * chans, chans))
    stats2 = exchange(moments)

    parts = 2
    while (bins + 2) % parts:
        parts -= 1
    folded = jnp.einsum("ijco,o->ijc", conv_second.astype(F32), out_proj, precision=lax.Precision.HIGHEST)
    mel_next, mel_in = pl.pallas_call(
        functools.partial(mel_kernel, bins, frames, count),
        out_shape=(jax.ShapeDtypeStruct((bins, frames), F32), jax.ShapeDtypeStruct((bins, lanes), BF16)),
        in_specs=[VMEM] * 2 + [pl.BlockSpec(memory_space=pl.ANY)] + [VMEM] * 4,
        out_specs=(VMEM,) * 2,
        scratch_shapes=[
            pltpu.VMEM(((bins + 4) * 8, lanes), F32),
            pltpu.VMEM((bins + 2, width, chans), BF16),
            pltpu.SemaphoreType.DMA((parts,)),
        ],
        compiler_params=pltpu.CompilerParams(vmem_limit_bytes=28 << 20),
        name="mel",
    )(stats2, small, first_out, folded, base, mel_noisy, stats)

    depth = pre_weight.shape[0]
    total, phases, outs = up_weight.shape
    weight = jnp.transpose(pre_weight, (1, 0, 2))
    quarters = fqs == 2 and lax.axis_size("song") == 2 and depth % 64 == 0
    if quarters:
        pieces = gather_slabs(weight, (right,), (moments,), (mel_in,))
    else:
        pieces = [after(lax.all_gather(weight, "tm", axis=0, tiled=False), mel_in)]
    slabs = 1
    while slabs * depth < 384 or tms % slabs:
        slabs += 1
    steps = tms // slabs
    if fqs == 2:
        mels = [mel_in, lax.ppermute(mel_in, "freq", swap)]
    else:
        mels = [lax.all_gather(mel_in, "freq", axis=0, tiled=True)]
    if quarters:
        steps = 4
        bias = pre_bias.reshape(tms, 4, depth // 4).swapaxes(0, 1).reshape(4, 1, total // 4)
        ready = [split_taps(up_weight, i, tms) for i in range(READY)]
    else:
        bias = pre_bias.reshape(steps, 1, total // steps)
        ready = []
    operands = mels + pieces + [bias, up_bias[None]]
    vocal = pl.pallas_call(
        functools.partial(up_kernel, frames, steps, fqs == 2, quarters),
        out_shape=jax.ShapeDtypeStruct((outs, 4 * frames), BF16),
        in_specs=[VMEM] * len(operands) + [pl.BlockSpec(memory_space=pl.ANY)] * (1 + len(ready)),
        out_specs=VMEM,
        scratch_shapes=[
            pltpu.VMEM((steps - len(ready), total // steps, phases, outs), BF16),
            pltpu.VMEM((steps - len(ready), outs // 128, total // steps * phases, 128), F32),
            pltpu.VMEM((max(len(ready), 1), phases, total // steps, outs), BF16),
            pltpu.SemaphoreType.DMA((steps, tms if quarters else 1)),
        ],
        compiler_params=pltpu.CompilerParams(vmem_limit_bytes=44 << 20),
        name="up",
    )(*operands, up_weight, *ready)
    return (mel_next, vocal)


def solution(mesh):
    in_specs = (
        P(None, "freq", ("song", "tm")),
        P("freq", ("song", "tm")),
        P("song"),
        P(),
        P(),
        P(),
        P(),
        P(),
        P(),
        P(),
        P(),
        P("tm", None, None),
        P(),
        P(None, None, "freq"),
        P("freq"),
    )
    out_specs = (P("freq", ("song", "tm")), P("freq", ("song", "tm")))
    return jax.shard_map(shards, mesh=mesh, in_specs=in_specs, out_specs=out_specs, check_vma=False)
```
